128 devices in a mesh: blk: 16 (over x, y_lo, core), rows: 8 (over z, y_hi).
Axes of the slice: x: 4, y: 4 (y_hi: 2, y_lo: 2; y = y_hi * 2 + y_lo), z: 4, core: 2. Of those that a mesh axis runs over, the one named last changes fastest.
Arguments:
- cholesky: bfloat16 [8192, 256, 256], P('blk', 'rows'), may hold values from -0.0078125 to 0.0078125
- green: bfloat16 [512, 256, 256], P('blk', 'rows'), may hold values from -18 to 18
- aux_field: float32 [512, 8192], P(None, 'blk'), may hold values from -6 to 6
- walker_orbitals: bfloat16 [512, 256, 128], P('blk', 'rows'), may hold values from -6 to 6
Outputs:
- new_orbitals: float32 [512, 256, 128], P('blk', 'rows')
- force_bias: float32 [512, 8192], P(None, 'blk')
The draws below stay inside these ranges and needn't reach their ends.
All inputs are finite; a program needn't handle non-finite values.
Results may differ from the reference program's by a relative error of at most 0.025.
Values may be sent and summed in bfloat16 or wider, within the bound.
A program may use at most 128 MiB of HBM per device.

```python
import jax
import jax.numpy as jnp
from jax import lax

N = 256
NOCC = 128
CH_DEV = 512
TAYLOR = 4
CHOL = 8192
WALKERS = 512
N_BLK = 16


def shard_levels(own_key, shape, cuts, least, largest):
    factor_of = 1.0
    for position, parts in cuts:
        steps = jax.random.uniform(jax.random.fold_in(jax.random.fold_in(own_key, 6), position), (parts,), jnp.float32, least / len(cuts), largest / len(cuts))
        factor_of = factor_of * jnp.repeat(jnp.exp(steps), shape[position] // parts).reshape((-1,) + (1,) * (len(shape) - 1 - position))
    return factor_of


def centred(key, dims, deviation, limit, cuts=(), kind=jnp.bfloat16):
    entries = deviation * jax.random.normal(key, dims, jnp.float32)
    if cuts:
        entries = entries * shard_levels(key, dims, cuts, -0.22, 0.18)
    return jnp.clip(entries, -limit, limit).astype(kind)


def setup_inputs(seed: int = 0) -> dict:
    keys = jax.random.split(jax.random.key(seed), 5)
    cholesky = centred(keys[0], (CHOL, N, N), (N * CHOL // 4) ** -0.5, 0.0078125, ((0, 16), (1, 8)))
    green = centred(keys[1], (WALKERS, N, N), 3.0, 18.0, ((0, 16), (1, 8)))
    aux_field = centred(keys[2], (WALKERS, CHOL), 1.0, 6.0, ((1, 16),), jnp.float32)
    walker_orbitals = centred(keys[3], (WALKERS, N, NOCC), 1.0, 6.0, ((0, 16), (1, 8)))
    return dict(cholesky=cholesky, green=green, aux_field=aux_field, walker_orbitals=walker_orbitals)


time_root = 0.5


def reference(cholesky, green, aux_field, walker_orbitals):
    flat_chol = cholesky.reshape(CHOL, N * N)
    flat_green = green.reshape(WALKERS, N * N)
    force_bias = lax.dot_general(flat_green, flat_chol, (((1,), (1,)), ((), ())), preferred_element_type=jnp.float32)
    shifted = (time_root * (aux_field - force_bias)).astype(jnp.bfloat16)

    def add_block(block, summed):
        first_vec = (block * CH_DEV).astype(jnp.int32)
        field_cols = lax.dynamic_slice_in_dim(shifted, first_vec, CH_DEV, 1)
        chol_rows = lax.dynamic_slice_in_dim(flat_chol, first_vec, CH_DEV, 0)
        partial_value = jnp.dot(field_cols, chol_rows, preferred_element_type=jnp.float32)
        return summed + partial_value.astype(jnp.bfloat16).astype(jnp.float32)

    summed = lax.fori_loop(0, N_BLK, add_block, jnp.zeros((WALKERS, N * N), jnp.float32))
    potential = summed.astype(jnp.bfloat16).reshape(WALKERS, N, N)
    taylor_term = walker_orbitals
    result = walker_orbitals.astype(jnp.float32)
    for degree in range(1, TAYLOR + 1):
        product = jnp.einsum("wik,wka->wia", potential.astype(jnp.float32), taylor_term.astype(jnp.float32))
        taylor_term = (product / degree).astype(jnp.bfloat16)
        result = result + taylor_term.astype(jnp.float32)
    return result, force_bias
```

```python
import jax
import jax.numpy as jnp
from jax import lax
from jax.experimental import pallas as pl
from jax.experimental.pallas import tpu as pltpu
from jax.sharding import PartitionSpec as P

TAYLOR = 4
MESH = pl.DeviceIdType.MESH
NQ = 2
BF = jnp.bfloat16
F32 = jnp.float32

POS = {2: 0, 1: 1, 3: 2, 0: 3}
OFFSETS = (2, 1, 3, 0)
PEERS = [(dz, dh) for dz in range(4) for dh in range(2) if (dz, dh) != (0, 0)]


def kernel(
    chol, green, aux, orbs, bias_out, delta_out,
    cn, gn, ch, gb, acc, part, rb, ff, ax, sh, pb,
    y_a, xp_b2, xm_b2, xp_b1, xm_b1, y_b, xp_a2, xm_a2, xp_a1, xm_a1,
    vn, vf, tf, res, send_sems, recv_sems, local_sems,
):
    vecs, rows, orbitals = chol.shape
    flat = rows * orbitals
    walk = green.shape[0] // NQ
    own_walk = walk // 8
    blk, row = lax.axis_index("blk"), lax.axis_index("rows")
    x, y, c = blk // 4, (blk // 2) % 2, blk % 2
    z, h = row // 2, row % 2

    def chip(dx, dy):
        return (lax.rem(x + dx, 4) * 4 + lax.rem(y + dy, 2) * 2 + c, row)

    def chip_index(dx, dy):
        return lax.rem(x + dx, 4) * 2 + lax.rem(y + dy, 2)

    def row_peer(dz, dh):
        return lax.rem(z + dz, 4) * 2 + lax.rem(h + dh, 2)

    right, left, across = chip(1, 0), chip(3, 0), chip(0, 1)
    partner = (x * 4 + y * 2 + (1 - c), row)

    a_half = flat * 7 // 32
    b_half = flat * 9 // 32
    a_all, b_all = 2 * a_half, 2 * b_half
    A1, A0, AA = pl.ds(0, a_half), pl.ds(a_half, a_half), pl.ds(0, a_all)
    B0, B1, BB = pl.ds(a_all, b_half), pl.ds(a_all + b_half, b_half), pl.ds(a_all, b_all)
    A0B0 = pl.ds(a_half, a_half + b_half)

    count = [0]
    sent = []

    def send(src, dst, device):
        k = count[0]
        count[0] += 1
        copy = pltpu.make_async_remote_copy(
            src_ref=src, dst_ref=dst, send_sem=send_sems.at[k], recv_sem=recv_sems.at[k],
            device_id=device, device_id_type=MESH,
        )
        copy.start()
        sent.append(copy)
        return copy

    local_count = [0]

    def local(src, dst):
        k = local_count[0]
        local_count[0] += 1
        copy = pltpu.make_async_copy(src, dst, local_sems.at[k])
        copy.start()
        return copy

    piece = cn.shape[1]
    pieces = vecs // piece
    green_in = local(green, gn)
    chol_in = {}

    def fetch(p):
        chol_in[p] = local(chol.at[pl.ds(p * piece, piece)], cn.at[p % 2])

    fetch(0)
    fetch(1)
    aux_in = local(aux.at[:, c], ax.at[0])
    orbs_in = local(orbs.at[:, row], tf.at[:, :, pl.ds(row * rows, rows)])

    barrier = pltpu.get_barrier_semaphore()
    greeted = [right, left, across, partner] + [(blk, row_peer(dz, dh)) for dz, dh in PEERS]
    for device in greeted:
        pl.semaphore_signal(barrier, inc=1, device_id=device, device_id_type=MESH)
    pl.semaphore_wait(barrier, len(greeted))

    gat = {}

    def gather_own(q):
        own = gb.at[q, POS[0], 0]
        own[...] = gn[pl.ds(q * walk, walk)].reshape(walk, flat)
        gat[q, "right"] = send(own, gb.at[q, POS[3], 0], right)
        gat[q, "left"] = send(own, gb.at[q, POS[1], 0], left)
        gat[q, "across"] = send(own, gb.at[q, POS[0], 1], across)

    def gather_near(q):
        gat[q, "across"].wait_recv()
        src = gb.at[q, POS[0], 1, :, BB]
        gat[q, "rightB"] = send(src, gb.at[q, POS[3], 1, :, BB], right)
        gat[q, "leftB"] = send(src, gb.at[q, POS[1], 1, :, BB], left)
        gat[q, "right"].wait_recv()
        near = gb.at[q, POS[3], 0]
        gat[q, "right2"] = send(near.at[:, A0B0], gb.at[q, POS[2], 0, :, A0B0], right)
        gat[q, "across3"] = send(near.at[:, AA], gb.at[q, POS[3], 1, :, AA], across)
        gat[q, "left"].wait_recv()
        near = gb.at[q, POS[1], 0]
        gat[q, "left2A"] = send(near.at[:, A1], gb.at[q, POS[2], 0, :, A1], left)
        gat[q, "left2B"] = send(near.at[:, B1], gb.at[q, POS[2], 0, :, B1], left)
        gat[q, "across1"] = send(near.at[:, AA], gb.at[q, POS[1], 1, :, AA], across)

    def gather_far(q):
        gat[q, "rightB"].wait_recv()
        gat[q, "right2B"] = send(gb.at[q, POS[3], 1, :, B0], gb.at[q, POS[2], 1, :, B0], right)
        gat[q, "leftB"].wait_recv()
        gat[q, "left2BB"] = send(gb.at[q, POS[1], 1, :, B1], gb.at[q, POS[2], 1, :, B1], left)
        gat[q, "right2"].wait_recv()
        gat[q, "across20"] = send(gb.at[q, POS[2], 0, :, A0], gb.at[q, POS[2], 1, :, A0], across)
        gat[q, "left2A"].wait_recv()
        gat[q, "across21"] = send(gb.at[q, POS[2], 0, :, A1], gb.at[q, POS[2], 1, :, A1], across)

    def gather_end(q):
        for name in ("left2B", "across3", "across1", "right2B", "left2BB", "across20", "across21"):
            gat[q, name].wait_recv()

    swaps = []

    def relayout(p):
        chol_in[p].wait()
        group = 16

        @pl.loop(0, piece // group)
        def _(s):
            at = pl.multiple_of(s * group, group)
            value = cn[p % 2, pl.ds(at, group)].reshape(group, flat)
            ch[pl.ds(pl.multiple_of(p * piece + at, group), group), :] = value

        swaps.append(
            send(ch.at[pl.ds(p * piece, piece)], ch.at[pl.ds(vecs + p * piece, piece)], partner)
        )
        if p + 2 < pieces:
            fetch(p + 2)

    depth = 4 * orbitals

    def bias_part(q, half):
        @pl.loop(0, flat // depth)
        def _(s):
            at = pl.ds(pl.multiple_of(s * depth, depth), depth)
            lhs = gb[q, :, :, :, at].reshape(8 * walk, depth)
            rhs = ch[pl.ds(half * vecs, vecs), at]
            product = lax.dot_general(
                lhs, rhs, (((1,), (1,)), ((), ())), preferred_element_type=F32
            )
            cols = pl.ds(half * vecs, vecs)
            first = jnp.where(s == 0, jnp.zeros_like(product), acc[:, cols])
            acc[:, cols] = first + product

    row_sent = {}

    def bias_send(q):
        for pos, dx in enumerate(OFFSETS):
            for dy in range(2):
                at = (pos * 2 + dy) * walk
                part[q, chip_index(dx, dy)] = acc[at : at + walk, :].astype(BF)
        for j, (dz, dh) in enumerate(PEERS):
            peer = row_peer(dz, dh)
            row_sent[q, "bias", j] = send(part.at[q, peer], rb.at[q, j], (blk, peer))

    def bias_sum(q):
        for j in range(len(PEERS)):
            row_sent[q, "bias", j].wait_recv()
        total = part[q, row].astype(F32)
        for j in range(len(PEERS)):
            total = total + rb[q, j].astype(F32)
        ff[q, row] = total.astype(BF)
        for j, (dz, dh) in enumerate(PEERS):
            row_sent[q, "sum", j] = send(ff.at[q, row], ff.at[q, row], (blk, row_peer(dz, dh)))

    outs = []

    def field(q):
        for j in range(len(PEERS)):
            row_sent[q, "sum", j].wait_recv()
        mine = pl.ds(q * walk, walk)
        outs.append(local(ff.at[q, :, :, pl.ds(0, vecs)], bias_out.at[:, c, mine]))
        row_sent[q, "out"] = send(
            ff.at[q, :, :, pl.ds(vecs, vecs)], bias_out.at[:, c, mine], partner
        )
        for pos, dx in enumerate(OFFSETS):
            for dy in range(2):
                j = chip_index(dx, dy)
                for half in range(2):
                    cols = pl.ds(half * vecs, vecs)
                    value = 0.5 * (ax[half, j, mine, :] - ff[q, j, :, cols].astype(F32))
                    at = (pos * 2 + dy) * walk
                    sh[q, at : at + walk, cols] = value.astype(BF)

    width = 2 * orbitals

    def potential(q, start, stop):
        @pl.loop(start // width, stop // width)
        def _(s):
            at = pl.ds(pl.multiple_of(s * width, width), width)
            product = jnp.dot(sh[q], ch[:, at], preferred_element_type=F32)
            pb[q, :, :, :, at] = product.astype(BF).reshape(4, 2, walk, width)

    red = {}

    def reduce_b(q):
        far = pb.at[q, POS[2]]
        red[q, "b2m"] = send(far.at[:, :, B0], xp_b2.at[q], left)
        red[q, "b2p"] = send(far.at[:, :, B1], xm_b2.at[q], right)
        near = pb.at[q, POS[3]]
        red[q, "b1m1"] = send(near.at[:, :, B1], xp_b1.at[q, :, :, pl.ds(b_half, b_half)], left)
        near = pb.at[q, POS[1]]
        red[q, "b1p0"] = send(near.at[:, :, B0], xm_b1.at[q, :, :, pl.ds(0, b_half)], right)

    def reduce_a(q):
        for name, lo, n in (("a2", 0, 1), ("a1", 1, 2), ("a0", 3, 1)):
            at = pl.ds(lo, n)
            red[q, name] = send(pb.at[q, at, 1, :, AA], y_a.at[q, at], across)

    def add(target, *terms):
        total = target[...].astype(F32)
        for term in terms:
            total = total + term[...].astype(F32)
        target[...] = total.astype(BF)

    def reduce_b_near(q):
        red[q, "b2m"].wait_recv()
        near = pb.at[q, POS[3], :, :, B0]
        add(near, xp_b2.at[q])
        red[q, "b1m0"] = send(near, xp_b1.at[q, :, :, pl.ds(0, b_half)], left)
        red[q, "b2p"].wait_recv()
        near = pb.at[q, POS[1], :, :, B1]
        add(near, xm_b2.at[q])
        red[q, "b1p1"] = send(near, xm_b1.at[q, :, :, pl.ds(b_half, b_half)], right)

    def reduce_a_far(q):
        red[q, "a2"].wait_recv()
        add(pb.at[q, POS[2], 0, :, AA], y_a.at[q, 0])
        far = pb.at[q, POS[2], 0]
        red[q, "a2m"] = send(far.at[:, A0], xp_a2.at[q], left)
        red[q, "a2p"] = send(far.at[:, A1], xm_a2.at[q], right)

    def reduce_a_near(q):
        red[q, "a1"].wait_recv()
        near = pb.at[q, POS[3], 0]
        add(near.at[:, A1], y_a.at[q, 2, :, A1])
        red[q, "a1m1"] = send(near.at[:, A1], xp_a1.at[q, :, A1], left)
        near = pb.at[q, POS[1], 0]
        add(near.at[:, A0], y_a.at[q, 1, :, A0])
        red[q, "a1p0"] = send(near.at[:, A0], xm_a1.at[q, :, A0], right)
        red[q, "a2m"].wait_recv()
        near = pb.at[q, POS[3], 0, :, A0]
        add(near, y_a.at[q, 2, :, A0], xp_a2.at[q])
        red[q, "a1m0"] = send(near, xp_a1.at[q, :, A0], left)
        red[q, "a2p"].wait_recv()
        near = pb.at[q, POS[1], 0, :, A1]
        add(near, y_a.at[q, 1, :, A1], xm_a2.at[q])
        red[q, "a1p1"] = send(near, xm_a1.at[q, :, A1], right)

    def reduce_b_across(q):
        for name in ("b1m0", "b1m1", "b1p0", "b1p1"):
            red[q, name].wait_recv()
        other = pb.at[q, POS[0], 1, :, BB]
        add(other, xp_b1.at[q, 1], xm_b1.at[q, 1])
        red[q, "b0"] = send(other, y_b.at[q], across)

    def reduce_end(q):
        own = pb.at[q, POS[0], 0]
        for name in ("a0", "a1m0", "a1m1", "a1p0", "a1p1"):
            red[q, name].wait_recv()
        add(own.at[:, AA], y_a.at[q, 3], xp_a1.at[q], xm_a1.at[q])
        red[q, "b0"].wait_recv()
        add(own.at[:, BB], xp_b1.at[q, 0], xm_b1.at[q, 0], y_b.at[q])
        vn[q] = own[...].reshape(walk, rows, orbitals)
        place = pl.ds(row * rows, rows)
        for j, (dz, dh) in enumerate(PEERS):
            peer = row_peer(dz, dh)
            red[q, "v", j] = send(
                vn.at[q, pl.ds(peer * own_walk, own_walk)], vf.at[q, :, place], (blk, peer)
            )
        vf[q, :, place] = vn[q, pl.ds(row * own_walk, own_walk)]

    def taylor(q):
        for j in range(len(PEERS)):
            red[q, "v", j].wait_recv()
        for w in range(own_walk):
            matrix = vf[q, w]
            term = tf[q, w]
            total = None
            for degree in range(1, TAYLOR + 1):
                product = jnp.dot(matrix, term, preferred_element_type=F32)
                term = (product / degree).astype(BF)
                wide = term.astype(F32)
                total = wide if total is None else total + wide
            res[q, w] = total.astype(BF)
        for j, (dz, dh) in enumerate(PEERS):
            peer = row_peer(dz, dh)
            red[q, "out", j] = send(
                res.at[q, :, pl.ds(peer * rows, rows)], delta_out.at[q, row], (blk, peer)
            )
        outs.append(local(res.at[q, :, pl.ds(row * rows, rows)], delta_out.at[q, row]))

    green_in.wait()
    gather_own(0)
    aux_swap = send(aux.at[:, 1 - c], ax.at[1], partner)
    relayout(0)
    relayout(1)
    gather_own(1)
    orb_sent = []
    for dz, dh in PEERS:
        peer = row_peer(dz, dh)
        orb_sent.append(
            send(orbs.at[:, peer], tf.at[:, :, pl.ds(row * rows, rows)], (blk, peer))
        )
    relayout(2)
    relayout(3)
    gather_near(0)
    relayout(4)
    relayout(5)
    gather_far(0)
    relayout(6)
    relayout(7)
    gather_near(1)
    gather_end(0)
    bias_part(0, 0)
    for copy in swaps:
        copy.wait_recv()
    bias_part(0, 1)
    bias_send(0)
    gather_far(1)
    bias_sum(0)
    aux_in.wait()
    aux_swap.wait_recv()
    field(0)
    potential(0, a_all, flat)
    reduce_b(0)
    potential(0, 0, a_all)
    reduce_a(0)
    gather_end(1)
    bias_part(1, 0)
    bias_part(1, 1)
    bias_send(1)
    reduce_b_near(0)
    reduce_a_far(0)
    bias_sum(1)
    reduce_a_near(0)
    field(1)
    potential(1, a_all, flat)
    reduce_b(1)
    potential(1, 0, a_all)
    reduce_a(1)
    reduce_b_across(0)
    reduce_b_near(1)
    reduce_a_far(1)
    reduce_end(0)
    orbs_in.wait()
    for copy in orb_sent:
        copy.wait_recv()
    reduce_a_near(1)
    taylor(0)
    reduce_b_across(1)
    reduce_end(1)
    taylor(1)
    for copy in outs:
        copy.wait()
    for q in range(NQ):
        row_sent[q, "out"].wait_recv()
        for j in range(len(PEERS)):
            red[q, "out", j].wait_recv()
    for copy in sent:
        copy.wait_send()


def shards(cholesky, green, aux_field, walker_orbitals):
    vecs, rows, orbitals = cholesky.shape
    walkers = green.shape[0]
    occupied = walker_orbitals.shape[2]
    flat = rows * orbitals
    walk = walkers // NQ
    own_walk = walk // 8
    a_all, b_all = flat * 7 // 16, flat * 9 // 16
    aux = aux_field.reshape(8, 2, walkers, vecs)
    orbs = walker_orbitals.reshape(NQ, 8, own_walk, rows, occupied)
    vmem = pltpu.VMEM
    scratch = [
        vmem((2, vecs // 8, rows, orbitals), BF),
        vmem((walkers, rows, orbitals), BF),
        vmem((2 * vecs, flat), BF),
        vmem((NQ, 4, 2, walk, flat), BF),
        vmem((8 * walk, 2 * vecs), F32),
        vmem((NQ, 8, walk, 2 * vecs), BF),
        vmem((NQ, 7, walk, 2 * vecs), BF),
        vmem((NQ, 8, walk, 2 * vecs), BF),
        vmem((2, 8, walkers, vecs), F32),
        vmem((NQ, 8 * walk, 2 * vecs), BF),
        vmem((NQ, 4, 2, walk, flat), BF),
        vmem((NQ, 4, walk, a_all), BF),
        vmem((NQ, 2, walk, b_all // 2), BF),
        vmem((NQ, 2, walk, b_all // 2), BF),
        vmem((NQ, 2, walk, b_all), BF),
        vmem((NQ, 2, walk, b_all), BF),
        vmem((NQ, walk, b_all), BF),
        vmem((NQ, walk, a_all // 2), BF),
        vmem((NQ, walk, a_all // 2), BF),
        vmem((NQ, walk, a_all), BF),
        vmem((NQ, walk, a_all), BF),
        vmem((NQ, walk, rows, orbitals), BF),
        vmem((NQ, own_walk, 8 * rows, orbitals), BF),
        vmem((NQ, own_walk, 8 * rows, occupied), BF),
        vmem((NQ, own_walk, 8 * rows, occupied), BF),
        pltpu.SemaphoreType.DMA((160,)),
        pltpu.SemaphoreType.DMA((160,)),
        pltpu.SemaphoreType.DMA((16,)),
    ]
    anywhere = pl.BlockSpec(memory_space=pl.ANY)
    bias, delta = pl.pallas_call(
        kernel,
        out_shape=(
            jax.ShapeDtypeStruct((8, 2, walkers, vecs), BF),
            jax.ShapeDtypeStruct(orbs.shape, BF),
        ),
        in_specs=[anywhere] * 4,
        out_specs=(anywhere, anywhere),
        scratch_shapes=scratch,
        compiler_params=pltpu.CompilerParams(
            collective_id=0, has_side_effects=True, vmem_limit_bytes=60 * 2**20
        ),
    )(cholesky, green, aux, orbs)
    result = walker_orbitals.astype(F32) + delta.reshape(walker_orbitals.shape).astype(F32)
    return result, bias.reshape(aux_field.shape).astype(F32)


def solution(mesh):
    return jax.shard_map(
        shards,
        mesh=mesh,
        in_specs=(
            P("blk", "rows", None),
            P("blk", "rows", None),
            P(None, "blk"),
            P("blk", "rows", None),
        ),
        out_specs=(P("blk", "rows", None), P(None, "blk")),
        check_vma=False,
    )
```

```python
import jax
import jax.numpy as jnp
from jax import lax
from jax.experimental import pallas as pl
from jax.experimental.pallas import tpu as pltpu
from jax.sharding import PartitionSpec as P

TAYLOR = 4
MESH = pl.DeviceIdType.MESH
NQ = 2
SHARE = 5
BF = jnp.bfloat16
F32 = jnp.float32

POS = {2: 0, 1: 1, 3: 2, 0: 3}
OFFSETS = (2, 1, 3, 0)
PEERS = [(dz, dh) for dz in range(4) for dh in range(2) if (dz, dh) != (0, 0)]


ORDER = (
    ("gather_own", 0),
    ("gather_across", 0),
    ("aux_send",),
    ("relayout", 0),
    ("relayout", 1),
    ("relayout", 2),
    ("relayout", 3),
    ("relayout", 4),
    ("relayout", 5),
    ("relayout", 6),
    ("relayout", 7),
    ("gather_turn", 0),
    ("gather_near", 0),
    ("orbitals_send",),
    ("gather_far", 0),
    ("gather_own", 1),
    ("gather_across", 1),
    ("gather_end", 0),
    ("swap_wait",),
    ("bias_send", 0),
    ("gather_turn", 1),
    ("gather_near", 1),
    ("bias_sum", 0),
    ("gather_far", 1),
    ("aux_wait",),
    ("gather_end", 1),
    ("bias_send", 1),
    ("field", 0),
    ("reduce_b", 0),
    ("potential_a", 0),
    ("bias_sum", 1),
    ("reduce_a", 0),
    ("reduce_b_near", 0),
    ("reduce_a_far", 0),
    ("field", 1),
    ("reduce_b", 1),
    ("potential_a", 1),
    ("reduce_a", 1),
    ("reduce_a_near", 0),
    ("reduce_b_across", 0),
    ("reduce_b_near", 1),
    ("reduce_a_far", 1),
    ("reduce_end", 0),
    ("orbitals_wait",),
    ("reduce_a_near", 1),
    ("taylor", 0),
    ("reduce_b_across", 1),
    ("reduce_end", 1),
    ("taylor", 1),
)


def kernel(
    chol, green, aux, orbs, bias_out, delta_out,
    cn, gn, ch, gb, part, rb, ff, ax, sh, pb,
    y_a, xp_b2, xm_b2, xp_b1, xm_b1, y_b, xp_a2, xm_a2, xp_a1, xm_a1,
    vn, vf, tf, res, send_sems, recv_sems, local_sems,
):
    vecs, rows, orbitals = chol.shape
    flat = rows * orbitals
    walk = green.shape[0] // NQ
    own_walk = walk // 8
    blk, row = lax.axis_index("blk"), lax.axis_index("rows")
    x, y, c = blk // 4, (blk // 2) % 2, blk % 2
    z, h = row // 2, row % 2

    def chip(dx, dy):
        return (lax.rem(x + dx, 4) * 4 + lax.rem(y + dy, 2) * 2 + c, row)

    def chip_index(dx, dy):
        return lax.rem(x + dx, 4) * 2 + lax.rem(y + dy, 2)

    def row_peer(dz, dh):
        return lax.rem(z + dz, 4) * 2 + lax.rem(h + dh, 2)

    right, left, across = chip(1, 0), chip(3, 0), chip(0, 1)
    partner = (x * 4 + y * 2 + (1 - c), row)

    a_half = flat * SHARE // 32
    b_half = flat * (16 - SHARE) // 32
    a_all, b_all = 2 * a_half, 2 * b_half
    A1, A0, AA = pl.ds(0, a_half), pl.ds(a_half, a_half), pl.ds(0, a_all)
    B0, B1, BB = pl.ds(a_all, b_half), pl.ds(a_all + b_half, b_half), pl.ds(a_all, b_all)
    A0B0 = pl.ds(a_half, a_half + b_half)

    count = [0]
    sent = []

    def send(src, dst, device):
        k = count[0]
        count[0] += 1
        copy = pltpu.make_async_remote_copy(
            src_ref=src, dst_ref=dst, send_sem=send_sems.at[k], recv_sem=recv_sems.at[k],
            device_id=device, device_id_type=MESH,
        )
        copy.start()
        sent.append(copy)
        return copy

    local_count = [0]

    def local(src, dst):
        k = local_count[0]
        local_count[0] += 1
        copy = pltpu.make_async_copy(src, dst, local_sems.at[k])
        copy.start()
        return copy

    piece = cn.shape[1]
    pieces = vecs // piece
    green_in = local(green, gn)
    chol_in = {}

    def fetch(p):
        chol_in[p] = local(chol.at[pl.ds(p * piece, piece)], cn.at[p])

    for p in range(pieces):
        fetch(p)
    aux_in = local(aux.at[:, c], ax.at[0])
    orbs_in = local(orbs.at[:, row], tf.at[:, :, pl.ds(row * rows, rows)])

    barrier = pltpu.get_barrier_semaphore()
    greeted = [right, left, across, partner] + [(blk, row_peer(dz, dh)) for dz, dh in PEERS]
    for device in greeted:
        pl.semaphore_signal(barrier, inc=1, device_id=device, device_id_type=MESH)
    green_in.wait()
    for q in range(NQ):
        gb[q, POS[0], 0] = gn[pl.ds(q * walk, walk)].reshape(walk, flat)
    pl.semaphore_wait(barrier, len(greeted))

    gat = {}

    def gather_own(q):
        own = gb.at[q, POS[0], 0]
        gat[q, "right"] = send(own, gb.at[q, POS[3], 0], right)
        gat[q, "left"] = send(own, gb.at[q, POS[1], 0], left)

    def gather_across(q):
        gat[q, "across"] = send(gb.at[q, POS[0], 0], gb.at[q, POS[0], 1], across)

    def gather_turn(q):
        gat[q, "across"].wait_recv()
        src = gb.at[q, POS[0], 1, :, BB]
        gat[q, "rightB"] = send(src, gb.at[q, POS[3], 1, :, BB], right)
        gat[q, "leftB"] = send(src, gb.at[q, POS[1], 1, :, BB], left)

    def gather_near(q):
        gat[q, "right"].wait_recv()
        near = gb.at[q, POS[3], 0]
        gat[q, "right2"] = send(near.at[:, A0B0], gb.at[q, POS[2], 0, :, A0B0], right)
        gat[q, "across3"] = send(near.at[:, AA], gb.at[q, POS[3], 1, :, AA], across)
        gat[q, "left"].wait_recv()
        near = gb.at[q, POS[1], 0]
        gat[q, "left2A"] = send(near.at[:, A1], gb.at[q, POS[2], 0, :, A1], left)
        gat[q, "left2B"] = send(near.at[:, B1], gb.at[q, POS[2], 0, :, B1], left)
        gat[q, "across1"] = send(near.at[:, AA], gb.at[q, POS[1], 1, :, AA], across)

    def gather_far(q):
        gat[q, "rightB"].wait_recv()
        gat[q, "right2B"] = send(gb.at[q, POS[3], 1, :, B0], gb.at[q, POS[2], 1, :, B0], right)
        gat[q, "leftB"].wait_recv()
        gat[q, "left2BB"] = send(gb.at[q, POS[1], 1, :, B1], gb.at[q, POS[2], 1, :, B1], left)
        gat[q, "right2"].wait_recv()
        gat[q, "across20"] = send(gb.at[q, POS[2], 0, :, A0], gb.at[q, POS[2], 1, :, A0], across)
        gat[q, "left2A"].wait_recv()
        gat[q, "across21"] = send(gb.at[q, POS[2], 0, :, A1], gb.at[q, POS[2], 1, :, A1], across)

    def gather_end(q):
        for name in ("left2B", "across3", "across1", "right2B", "left2BB", "across20", "across21"):
            gat[q, name].wait_recv()

    swaps = []

    def relayout(p):
        chol_in[p].wait()
        group = 16

        @pl.loop(0, piece // group)
        def _(s):
            at = pl.multiple_of(s * group, group)
            value = cn[p, pl.ds(at, group)].reshape(group, flat)
            ch[pl.ds(pl.multiple_of(p * piece + at, group), group), :] = value

        swaps.append(
            send(ch.at[pl.ds(p * piece, piece)], ch.at[pl.ds(vecs + p * piece, piece)], partner)
        )

    row_sent = {}

    def bias_send(q):
        product = lax.dot_general(
            gb[q].reshape(8 * walk, flat), ch[...], (((1,), (1,)), ((), ())),
            preferred_element_type=F32,
        )
        for pos, dx in enumerate(OFFSETS):
            for dy in range(2):
                at = (pos * 2 + dy) * walk
                part[q, chip_index(dx, dy)] = product[at : at + walk, :].astype(BF)
        for j, (dz, dh) in enumerate(PEERS):
            peer = row_peer(dz, dh)
            row_sent[q, "bias", j] = send(part.at[q, peer], rb.at[q, j], (blk, peer))

    def bias_sum(q):
        for j in range(len(PEERS)):
            row_sent[q, "bias", j].wait_recv()
        total = part[q, row].astype(F32)
        for j in range(len(PEERS)):
            total = total + rb[q, j].astype(F32)
        ff[q, row] = total.astype(BF)
        for j, (dz, dh) in enumerate(PEERS):
            row_sent[q, "sum", j] = send(ff.at[q, row], ff.at[q, row], (blk, row_peer(dz, dh)))

    outs = []

    def field(q):
        for j in range(len(PEERS)):
            row_sent[q, "sum", j].wait_recv()
        mine = pl.ds(q * walk, walk)
        outs.append(local(ff.at[q, :, :, pl.ds(0, vecs)], bias_out.at[:, c, mine]))
        row_sent[q, "out"] = send(
            ff.at[q, :, :, pl.ds(vecs, vecs)], bias_out.at[:, c, mine], partner
        )
        for pos, dx in enumerate(OFFSETS):
            for dy in range(2):
                j = chip_index(dx, dy)
                for half in range(2):
                    cols = pl.ds(half * vecs, vecs)
                    value = 0.5 * (ax[half, j, mine, :] - ff[q, j, :, cols].astype(F32))
                    at = (pos * 2 + dy) * walk
                    sh[q, at : at + walk, cols] = value.astype(BF)

    def potential(q, at):
        product = jnp.dot(sh[q], ch[:, at], preferred_element_type=F32)
        pb[q, :, :, :, at] = product.astype(BF).reshape(4, 2, walk, at.size)

    red = {}

    def reduce_b(q):
        potential(q, B0)
        red[q, "b2m"] = send(pb.at[q, POS[2], :, :, B0], xp_b2.at[q], left)
        at = pl.ds(0, b_half)
        red[q, "b1p0"] = send(pb.at[q, POS[1], :, :, B0], xm_b1.at[q, :, :, at], right)
        potential(q, B1)
        red[q, "b2p"] = send(pb.at[q, POS[2], :, :, B1], xm_b2.at[q], right)
        at = pl.ds(b_half, b_half)
        red[q, "b1m1"] = send(pb.at[q, POS[3], :, :, B1], xp_b1.at[q, :, :, at], left)

    def reduce_a(q):
        for name, lo, n in (("a2", 0, 1), ("a1", 1, 2), ("a0", 3, 1)):
            at = pl.ds(lo, n)
            red[q, name] = send(pb.at[q, at, 1, :, AA], y_a.at[q, at], across)

    def add(target, *terms):
        total = target[...].astype(F32)
        for term in terms:
            total = total + term[...].astype(F32)
        target[...] = total.astype(BF)

    def reduce_b_near(q):
        red[q, "b2m"].wait_recv()
        near = pb.at[q, POS[3], :, :, B0]
        add(near, xp_b2.at[q])
        red[q, "b1m0"] = send(near, xp_b1.at[q, :, :, pl.ds(0, b_half)], left)
        red[q, "b2p"].wait_recv()
        near = pb.at[q, POS[1], :, :, B1]
        add(near, xm_b2.at[q])
        red[q, "b1p1"] = send(near, xm_b1.at[q, :, :, pl.ds(b_half, b_half)], right)

    def reduce_a_far(q):
        red[q, "a2"].wait_recv()
        add(pb.at[q, POS[2], 0, :, AA], y_a.at[q, 0])
        far = pb.at[q, POS[2], 0]
        red[q, "a2m"] = send(far.at[:, A0], xp_a2.at[q], left)
        red[q, "a2p"] = send(far.at[:, A1], xm_a2.at[q], right)

    def reduce_a_near(q):
        red[q, "a1"].wait_recv()
        near = pb.at[q, POS[3], 0]
        add(near.at[:, A1], y_a.at[q, 2, :, A1])
        red[q, "a1m1"] = send(near.at[:, A1], xp_a1.at[q, :, A1], left)
        near = pb.at[q, POS[1], 0]
        add(near.at[:, A0], y_a.at[q, 1, :, A0])
        red[q, "a1p0"] = send(near.at[:, A0], xm_a1.at[q, :, A0], right)
        red[q, "a2m"].wait_recv()
        near = pb.at[q, POS[3], 0, :, A0]
        add(near, y_a.at[q, 2, :, A0], xp_a2.at[q])
        red[q, "a1m0"] = send(near, xp_a1.at[q, :, A0], left)
        red[q, "a2p"].wait_recv()
        near = pb.at[q, POS[1], 0, :, A1]
        add(near, y_a.at[q, 1, :, A1], xm_a2.at[q])
        red[q, "a1p1"] = send(near, xm_a1.at[q, :, A1], right)

    def reduce_b_across(q):
        for name in ("b1m0", "b1m1", "b1p0", "b1p1"):
            red[q, name].wait_recv()
        other = pb.at[q, POS[0], 1, :, BB]
        add(other, xp_b1.at[q, 1], xm_b1.at[q, 1])
        red[q, "b0"] = send(other, y_b.at[q], across)

    def reduce_end(q):
        own = pb.at[q, POS[0], 0]
        for name in ("a0", "a1m0", "a1m1", "a1p0", "a1p1"):
            red[q, name].wait_recv()
        add(own.at[:, AA], y_a.at[q, 3], xp_a1.at[q], xm_a1.at[q])
        red[q, "b0"].wait_recv()
        add(own.at[:, BB], xp_b1.at[q, 0], xm_b1.at[q, 0], y_b.at[q])
        vn[q] = own[...].reshape(walk, rows, orbitals)
        place = pl.ds(row * rows, rows)
        for j, (dz, dh) in enumerate(PEERS):
            peer = row_peer(dz, dh)
            red[q, "v", j] = send(
                vn.at[q, pl.ds(peer * own_walk, own_walk)], vf.at[q, :, place], (blk, peer)
            )
        vf[q, :, place] = vn[q, pl.ds(row * own_walk, own_walk)]

    def taylor(q):
        for j in range(len(PEERS)):
            red[q, "v", j].wait_recv()
        term = [tf[q, w] for w in range(own_walk)]
        total = [None] * own_walk
        for degree in range(1, TAYLOR + 1):
            for w in range(own_walk):
                product = jnp.dot(vf[q, w], term[w], preferred_element_type=F32)
                term[w] = (product / degree).astype(BF)
                wide = term[w].astype(F32)
                total[w] = wide if degree == 1 else total[w] + wide
        for w in range(own_walk):
            res[q, w] = total[w].astype(BF)
        for j, (dz, dh) in enumerate(PEERS):
            peer = row_peer(dz, dh)
            red[q, "out", j] = send(
                res.at[q, :, pl.ds(peer * rows, rows)], delta_out.at[q, row], (blk, peer)
            )
        outs.append(local(res.at[q, :, pl.ds(row * rows, rows)], delta_out.at[q, row]))

    orb_sent = []

    def orbitals_send():
        for dz, dh in PEERS:
            peer = row_peer(dz, dh)
            orb_sent.append(
                send(orbs.at[:, peer], tf.at[:, :, pl.ds(row * rows, rows)], (blk, peer))
            )

    def orbitals_wait():
        orbs_in.wait()
        for copy in orb_sent:
            copy.wait_recv()

    def swap_wait():
        for copy in swaps:
            copy.wait_recv()

    aux_swap = []

    def aux_send():
        aux_swap.append(send(aux.at[:, 1 - c], ax.at[1], partner))

    def aux_wait():
        aux_in.wait()
        aux_swap[0].wait_recv()

    steps = dict(
        gather_own=gather_own, gather_across=gather_across, gather_turn=gather_turn, gather_near=gather_near, gather_far=gather_far,
        gather_end=gather_end, relayout=relayout, swap_wait=swap_wait, aux_send=aux_send,
        aux_wait=aux_wait, orbitals_send=orbitals_send, orbitals_wait=orbitals_wait,
        bias_send=bias_send, bias_sum=bias_sum, field=field,
        potential_a=lambda q: potential(q, AA),
        reduce_b=reduce_b, reduce_a=reduce_a, reduce_b_near=reduce_b_near,
        reduce_a_far=reduce_a_far, reduce_a_near=reduce_a_near,
        reduce_b_across=reduce_b_across, reduce_end=reduce_end, taylor=taylor,
    )
    for name, *where in ORDER:
        steps[name](*where)
    for copy in outs:
        copy.wait()
    for q in range(NQ):
        row_sent[q, "out"].wait_recv()
        for j in range(len(PEERS)):
            red[q, "out", j].wait_recv()
    for copy in sent:
        copy.wait_send()


def shards(cholesky, green, aux_field, walker_orbitals):
    vecs, rows, orbitals = cholesky.shape
    walkers = green.shape[0]
    occupied = walker_orbitals.shape[2]
    flat = rows * orbitals
    walk = walkers // NQ
    own_walk = walk // 8
    a_all, b_all = flat * SHARE // 16, flat * (16 - SHARE) // 16
    aux = aux_field.reshape(8, 2, walkers, vecs)
    orbs = walker_orbitals.reshape(NQ, 8, own_walk, rows, occupied)
    vmem = pltpu.VMEM
    scratch = [
        vmem((8, vecs // 8, rows, orbitals), BF),
        vmem((walkers, rows, orbitals), BF),
        vmem((2 * vecs, flat), BF),
        vmem((NQ, 4, 2, walk, flat), BF),
        vmem((NQ, 8, walk, 2 * vecs), BF),
        vmem((NQ, 7, walk, 2 * vecs), BF),
        vmem((NQ, 8, walk, 2 * vecs), BF),
        vmem((2, 8, walkers, vecs), F32),
        vmem((NQ, 8 * walk, 2 * vecs), BF),
        vmem((NQ, 4, 2, walk, flat), BF),
        vmem((NQ, 4, walk, a_all), BF),
        vmem((NQ, 2, walk, b_all // 2), BF),
        vmem((NQ, 2, walk, b_all // 2), BF),
        vmem((NQ, 2, walk, b_all), BF),
        vmem((NQ, 2, walk, b_all), BF),
        vmem((NQ, walk, b_all), BF),
        vmem((NQ, walk, a_all // 2), BF),
        vmem((NQ, walk, a_all // 2), BF),
        vmem((NQ, walk, a_all), BF),
        vmem((NQ, walk, a_all), BF),
        vmem((NQ, walk, rows, orbitals), BF),
        vmem((NQ, own_walk, 8 * rows, orbitals), BF),
        vmem((NQ, own_walk, 8 * rows, occupied), BF),
        vmem((NQ, own_walk, 8 * rows, occupied), BF),
        pltpu.SemaphoreType.DMA((160,)),
        pltpu.SemaphoreType.DMA((160,)),
        pltpu.SemaphoreType.DMA((16,)),
    ]
    anywhere = pl.BlockSpec(memory_space=pl.ANY)
    bias, delta = pl.pallas_call(
        kernel,
        out_shape=(
            jax.ShapeDtypeStruct((8, 2, walkers, vecs), BF),
            jax.ShapeDtypeStruct(orbs.shape, BF),
        ),
        in_specs=[anywhere] * 4,
        out_specs=(anywhere, anywhere),
        scratch_shapes=scratch,
        compiler_params=pltpu.CompilerParams(
            collective_id=0, has_side_effects=True, vmem_limit_bytes=60 * 2**20
        ),
    )(cholesky, green, aux, orbs)
    result = walker_orbitals.astype(F32) + delta.reshape(walker_orbitals.shape).astype(F32)
    return result, bias.reshape(aux_field.shape).astype(F32)


def solution(mesh):
    return jax.shard_map(
        shards,
        mesh=mesh,
        in_specs=(
            P("blk", "rows", None),
            P("blk", "rows", None),
            P(None, "blk"),
            P("blk", "rows", None),
        ),
        out_specs=(P("blk", "rows", None), P(None, "blk")),
        check_vma=False,
    )
```

```python
import jax
import jax.numpy as jnp
from jax import lax
from jax.experimental import pallas as pl
from jax.experimental.pallas import tpu as pltpu
from jax.sharding import PartitionSpec as P

TAYLOR = 4
MESH = pl.DeviceIdType.MESH
NQ = 2
SHARE = 4
BF = jnp.bfloat16
F32 = jnp.float32

POS = {2: 0, 1: 1, 3: 2, 0: 3}
OFFSETS = (2, 1, 3, 0)
PEERS = [(dz, dh) for dz in range(4) for dh in range(2) if (dz, dh) != (0, 0)]


ORDER = (
    ("gather_own", 0),
    ("gather_across", 0),
    ("fetch_all",),
    ("aux_send",),
    ("relayout", 0),
    ("relayout", 1),
    ("relayout", 2),
    ("relayout", 3),
    ("relayout", 4),
    ("relayout", 5),
    ("relayout", 6),
    ("relayout", 7),
    ("gather_turn", 0),
    ("gather_near", 0),
    ("gather_far", 0),
    ("gather_own", 1),
    ("gather_across", 1),
    ("gather_end", 0),
    ("swap_wait",),
    ("bias_send", 0),
    ("gather_turn", 1),
    ("gather_near", 1),
    ("bias_sum", 0),
    ("gather_far", 1),
    ("aux_wait",),
    ("gather_end", 1),
    ("bias_send", 1),
    ("orbitals_send",),
    ("field", 0),
    ("reduce_b", 0),
    ("potential_a", 0),
    ("bias_sum", 1),
    ("reduce_a", 0),
    ("reduce_b_near", 0),
    ("reduce_a_far", 0),
    ("field", 1),
    ("reduce_b", 1),
    ("potential_a", 1),
    ("reduce_a", 1),
    ("reduce_a_near", 0),
    ("reduce_b_across", 0),
    ("reduce_b_near", 1),
    ("reduce_a_far", 1),
    ("reduce_end", 0),
    ("orbitals_wait",),
    ("reduce_b_across", 1),
    ("reduce_a_near", 1),
    ("taylor", 0),
    ("reduce_end", 1),
    ("taylor", 1),
)


def kernel(
    chol, green, aux, orbs, bias_out, delta_out,
    cn, gn, ch, gb, part, rb, ff, ax, sh, pb,
    y_a, xp_b2, xm_b2, xp_b1, xm_b1, y_b, xp_a2, xm_a2, xp_a1, xm_a1,
    vn, vf, tf, res, send_sems, recv_sems, local_sems,
):
    vecs, rows, orbitals = chol.shape
    flat = rows * orbitals
    walk = green.shape[0] // NQ
    own_walk = walk // 8
    blk, row = lax.axis_index("blk"), lax.axis_index("rows")
    x, y, c = blk // 4, (blk // 2) % 2, blk % 2
    z, h = row // 2, row % 2

    def chip(dx, dy):
        return (lax.rem(x + dx, 4) * 4 + lax.rem(y + dy, 2) * 2 + c, row)

    def chip_index(dx, dy):
        return lax.rem(x + dx, 4) * 2 + lax.rem(y + dy, 2)

    def row_peer(dz, dh):
        return lax.rem(z + dz, 4) * 2 + lax.rem(h + dh, 2)

    right, left, across = chip(1, 0), chip(3, 0), chip(0, 1)
    partner = (x * 4 + y * 2 + (1 - c), row)

    a_half = flat * SHARE // 32
    b_half = flat * (16 - SHARE) // 32
    a_all, b_all = 2 * a_half, 2 * b_half
    A1, A0, AA = pl.ds(0, a_half), pl.ds(a_half, a_half), pl.ds(0, a_all)
    B0, B1, BB = pl.ds(a_all, b_half), pl.ds(a_all + b_half, b_half), pl.ds(a_all, b_all)
    A0B0 = pl.ds(a_half, a_half + b_half)

    count = [0]
    sent = []

    def send(src, dst, device):
        k = count[0]
        count[0] += 1
        copy = pltpu.make_async_remote_copy(
            src_ref=src, dst_ref=dst, send_sem=send_sems.at[k], recv_sem=recv_sems.at[k],
            device_id=device, device_id_type=MESH,
        )
        copy.start()
        sent.append(copy)
        return copy

    local_count = [0]

    def local(src, dst):
        k = local_count[0]
        local_count[0] += 1
        copy = pltpu.make_async_copy(src, dst, local_sems.at[k])
        copy.start()
        return copy

    piece = cn.shape[1]
    pieces = vecs // piece
    green_in = local(green, gn)
    chol_in, fetched = {}, {}

    def fetch(p):
        chol_in[p] = local(chol.at[pl.ds(p * piece, piece)], cn.at[p])

    barrier = pltpu.get_barrier_semaphore()
    greeted = [right, left, across, partner] + [(blk, row_peer(dz, dh)) for dz, dh in PEERS]
    for device in greeted:
        pl.semaphore_signal(barrier, inc=1, device_id=device, device_id_type=MESH)
    green_in.wait()
    for q in range(NQ):
        gb[q, POS[0], 0] = gn[pl.ds(q * walk, walk)].reshape(walk, flat)
    pl.semaphore_wait(barrier, len(greeted))

    gat = {}

    def gather_own(q):
        own = gb.at[q, POS[0], 0]
        gat[q, "right"] = send(own, gb.at[q, POS[3], 0], right)
        gat[q, "left"] = send(own, gb.at[q, POS[1], 0], left)

    def gather_across(q):
        gat[q, "across"] = send(gb.at[q, POS[0], 0], gb.at[q, POS[0], 1], across)

    def gather_turn(q):
        gat[q, "across"].wait_recv()
        src = gb.at[q, POS[0], 1, :, BB]
        gat[q, "rightB"] = send(src, gb.at[q, POS[3], 1, :, BB], right)
        gat[q, "leftB"] = send(src, gb.at[q, POS[1], 1, :, BB], left)

    def gather_near(q):
        gat[q, "right"].wait_recv()
        near = gb.at[q, POS[3], 0]
        gat[q, "right2"] = send(near.at[:, A0B0], gb.at[q, POS[2], 0, :, A0B0], right)
        gat[q, "across3"] = send(near.at[:, AA], gb.at[q, POS[3], 1, :, AA], across)
        gat[q, "left"].wait_recv()
        near = gb.at[q, POS[1], 0]
        gat[q, "left2A"] = send(near.at[:, A1], gb.at[q, POS[2], 0, :, A1], left)
        gat[q, "left2B"] = send(near.at[:, B1], gb.at[q, POS[2], 0, :, B1], left)
        gat[q, "across1"] = send(near.at[:, AA], gb.at[q, POS[1], 1, :, AA], across)

    def gather_far(q):
        gat[q, "rightB"].wait_recv()
        gat[q, "right2B"] = send(gb.at[q, POS[3], 1, :, B0], gb.at[q, POS[2], 1, :, B0], right)
        gat[q, "leftB"].wait_recv()
        gat[q, "left2BB"] = send(gb.at[q, POS[1], 1, :, B1], gb.at[q, POS[2], 1, :, B1], left)
        gat[q, "right2"].wait_recv()
        gat[q, "across20"] = send(gb.at[q, POS[2], 0, :, A0], gb.at[q, POS[2], 1, :, A0], across)
        gat[q, "left2A"].wait_recv()
        gat[q, "across21"] = send(gb.at[q, POS[2], 0, :, A1], gb.at[q, POS[2], 1, :, A1], across)

    def gather_end(q):
        for name in ("left2B", "across3", "across1", "right2B", "left2BB", "across20", "across21"):
            gat[q, name].wait_recv()

    swaps = []

    def relayout(p):
        chol_in[p].wait()
        group = 16

        @pl.loop(0, piece // group)
        def _(s):
            at = pl.multiple_of(s * group, group)
            value = cn[p, pl.ds(at, group)].reshape(group, flat)
            ch[pl.ds(pl.multiple_of(p * piece + at, group), group), :] = value

        swaps.append(
            send(ch.at[pl.ds(p * piece, piece)], ch.at[pl.ds(vecs + p * piece, piece)], partner)
        )

    row_sent = {}

    def bias_send(q):
        product = lax.dot_general(
            gb[q].reshape(8 * walk, flat), ch[...], (((1,), (1,)), ((), ())),
            preferred_element_type=F32,
        )
        for pos, dx in enumerate(OFFSETS):
            for dy in range(2):
                at = (pos * 2 + dy) * walk
                part[q, chip_index(dx, dy)] = product[at : at + walk, :].astype(BF)
        for j, (dz, dh) in enumerate(PEERS):
            peer = row_peer(dz, dh)
            row_sent[q, "bias", j] = send(part.at[q, peer], rb.at[q, j], (blk, peer))

    def bias_sum(q):
        for j in range(len(PEERS)):
            row_sent[q, "bias", j].wait_recv()
        total = part[q, row].astype(F32)
        for j in range(len(PEERS)):
            total = total + rb[q, j].astype(F32)
        ff[q, row] = total.astype(BF)
        for j, (dz, dh) in enumerate(PEERS):
            row_sent[q, "sum", j] = send(ff.at[q, row], ff.at[q, row], (blk, row_peer(dz, dh)))

    outs = []

    def field(q):
        for j in range(len(PEERS)):
            row_sent[q, "sum", j].wait_recv()
        mine = pl.ds(q * walk, walk)
        outs.append(local(ff.at[q, :, :, pl.ds(0, vecs)], bias_out.at[:, c, mine]))
        row_sent[q, "out"] = send(
            ff.at[q, :, :, pl.ds(vecs, vecs)], bias_out.at[:, c, mine], partner
        )
        for pos, dx in enumerate(OFFSETS):
            for dy in range(2):
                j = chip_index(dx, dy)
                for half in range(2):
                    cols = pl.ds(half * vecs, vecs)
                    value = 0.5 * (ax[half, j, mine, :] - ff[q, j, :, cols].astype(F32))
                    at = (pos * 2 + dy) * walk
                    sh[q, at : at + walk, cols] = value.astype(BF)

    def potential(q, at):
        product = jnp.dot(sh[q], ch[:, at], preferred_element_type=F32)
        pb[q, :, :, :, at] = product.astype(BF).reshape(4, 2, walk, at.size)

    red = {}

    def reduce_b(q):
        potential(q, B0)
        red[q, "b2m"] = send(pb.at[q, POS[2], :, :, B0], xp_b2.at[q], left)
        at = pl.ds(0, b_half)
        red[q, "b1p0"] = send(pb.at[q, POS[1], :, :, B0], xm_b1.at[q, :, :, at], right)
        potential(q, B1)
        red[q, "b2p"] = send(pb.at[q, POS[2], :, :, B1], xm_b2.at[q], right)
        at = pl.ds(b_half, b_half)
        red[q, "b1m1"] = send(pb.at[q, POS[3], :, :, B1], xp_b1.at[q, :, :, at], left)

    def reduce_a(q):
        for name, lo, n in (("a2", 0, 1), ("a1", 1, 2), ("a0", 3, 1)):
            at = pl.ds(lo, n)
            red[q, name] = send(pb.at[q, at, 1, :, AA], y_a.at[q, at], across)

    def add(target, *terms):
        total = target[...].astype(F32)
        for term in terms:
            total = total + term[...].astype(F32)
        target[...] = total.astype(BF)

    def reduce_b_near(q):
        red[q, "b2m"].wait_recv()
        near = pb.at[q, POS[3], :, :, B0]
        add(near, xp_b2.at[q])
        red[q, "b1m0"] = send(near, xp_b1.at[q, :, :, pl.ds(0, b_half)], left)
        red[q, "b2p"].wait_recv()
        near = pb.at[q, POS[1], :, :, B1]
        add(near, xm_b2.at[q])
        red[q, "b1p1"] = send(near, xm_b1.at[q, :, :, pl.ds(b_half, b_half)], right)

    def reduce_a_far(q):
        red[q, "a2"].wait_recv()
        add(pb.at[q, POS[2], 0, :, AA], y_a.at[q, 0])
        far = pb.at[q, POS[2], 0]
        red[q, "a2m"] = send(far.at[:, A0], xp_a2.at[q], left)
        red[q, "a2p"] = send(far.at[:, A1], xm_a2.at[q], right)

    def reduce_a_near(q):
        red[q, "a1"].wait_recv()
        near = pb.at[q, POS[3], 0]
        add(near.at[:, A1], y_a.at[q, 2, :, A1])
        red[q, "a1m1"] = send(near.at[:, A1], xp_a1.at[q, :, A1], left)
        near = pb.at[q, POS[1], 0]
        add(near.at[:, A0], y_a.at[q, 1, :, A0])
        red[q, "a1p0"] = send(near.at[:, A0], xm_a1.at[q, :, A0], right)
        red[q, "a2m"].wait_recv()
        near = pb.at[q, POS[3], 0, :, A0]
        add(near, y_a.at[q, 2, :, A0], xp_a2.at[q])
        red[q, "a1m0"] = send(near, xp_a1.at[q, :, A0], left)
        red[q, "a2p"].wait_recv()
        near = pb.at[q, POS[1], 0, :, A1]
        add(near, y_a.at[q, 1, :, A1], xm_a2.at[q])
        red[q, "a1p1"] = send(near, xm_a1.at[q, :, A1], right)

    def reduce_b_across(q):
        for name in ("b1m0", "b1m1", "b1p0", "b1p1"):
            red[q, name].wait_recv()
        other = pb.at[q, POS[0], 1, :, BB]
        add(other, xp_b1.at[q, 1], xm_b1.at[q, 1])
        red[q, "b0"] = send(other, y_b.at[q], across)

    def reduce_end(q):
        own = pb.at[q, POS[0], 0]
        for name in ("a0", "a1m0", "a1m1", "a1p0", "a1p1"):
            red[q, name].wait_recv()
        add(own.at[:, AA], y_a.at[q, 3], xp_a1.at[q], xm_a1.at[q])
        red[q, "b0"].wait_recv()
        add(own.at[:, BB], xp_b1.at[q, 0], xm_b1.at[q, 0], y_b.at[q])
        vn[q] = own[...].reshape(walk, rows, orbitals)
        place = pl.ds(row * rows, rows)
        for j, (dz, dh) in enumerate(PEERS):
            peer = row_peer(dz, dh)
            red[q, "v", j] = send(
                vn.at[q, pl.ds(peer * own_walk, own_walk)], vf.at[q, :, place], (blk, peer)
            )
        vf[q, :, place] = vn[q, pl.ds(row * own_walk, own_walk)]

    def taylor(q):
        for j in range(len(PEERS)):
            red[q, "v", j].wait_recv()
        term = [tf[q, w] for w in range(own_walk)]
        total = [None] * own_walk
        for degree in range(1, TAYLOR + 1):
            for w in range(own_walk):
                product = jnp.dot(vf[q, w], term[w], preferred_element_type=F32)
                term[w] = (product / degree).astype(BF)
                wide = term[w].astype(F32)
                total[w] = wide if degree == 1 else total[w] + wide
        for w in range(own_walk):
            res[q, w] = total[w].astype(BF)
        for j, (dz, dh) in enumerate(PEERS):
            peer = row_peer(dz, dh)
            red[q, "out", j] = send(
                res.at[q, :, pl.ds(peer * rows, rows)], delta_out.at[q, row], (blk, peer)
            )
        outs.append(local(res.at[q, :, pl.ds(row * rows, rows)], delta_out.at[q, row]))

    orb_sent = []

    def orbitals_send():
        for dz, dh in PEERS:
            peer = row_peer(dz, dh)
            orb_sent.append(
                send(orbs.at[:, peer], tf.at[:, :, pl.ds(row * rows, rows)], (blk, peer))
            )

    def orbitals_wait():
        fetched["orbs"].wait()
        for copy in orb_sent:
            copy.wait_recv()

    def swap_wait():
        for copy in swaps:
            copy.wait_recv()

    aux_swap = []

    def aux_send():
        aux_swap.append(send(aux.at[:, 1 - c], ax.at[1], partner))

    def aux_wait():
        fetched["aux"].wait()
        aux_swap[0].wait_recv()

    def fetch_all():
        for p in range(pieces):
            fetch(p)
        fetched["aux"] = local(aux.at[:, c], ax.at[0])
        fetched["orbs"] = local(orbs.at[:, row], tf.at[:, :, pl.ds(row * rows, rows)])

    steps = dict(
        fetch_all=fetch_all,
        gather_own=gather_own, gather_across=gather_across, gather_turn=gather_turn, gather_near=gather_near, gather_far=gather_far,
        gather_end=gather_end, relayout=relayout, swap_wait=swap_wait, aux_send=aux_send,
        aux_wait=aux_wait, orbitals_send=orbitals_send, orbitals_wait=orbitals_wait,
        bias_send=bias_send, bias_sum=bias_sum, field=field,
        potential_a=lambda q: potential(q, AA),
        reduce_b=reduce_b, reduce_a=reduce_a, reduce_b_near=reduce_b_near,
        reduce_a_far=reduce_a_far, reduce_a_near=reduce_a_near,
        reduce_b_across=reduce_b_across, reduce_end=reduce_end, taylor=taylor,
    )
    for name, *where in ORDER:
        steps[name](*where)
    for copy in outs:
        copy.wait()
    for q in range(NQ):
        row_sent[q, "out"].wait_recv()
        for j in range(len(PEERS)):
            red[q, "out", j].wait_recv()
    for copy in sent:
        copy.wait_send()


def widen_kernel(orbs, delta, bias, result, wide):
    result[...] = orbs[...].astype(F32) + delta[...].astype(F32)
    wide[...] = bias[...].astype(F32)


def widen(orbs, delta, bias, steps=4):
    part = pl.BlockSpec((orbs.shape[0] // steps, *orbs.shape[1:]), lambda i: (i, 0, 0))
    flat = pl.BlockSpec((bias.shape[0] // steps, bias.shape[1]), lambda i: (i, 0))
    return pl.pallas_call(
        widen_kernel,
        grid=(steps,),
        out_shape=(
            jax.ShapeDtypeStruct(orbs.shape, F32), jax.ShapeDtypeStruct(bias.shape, F32),
        ),
        in_specs=[part, part, flat],
        out_specs=(part, flat),
    )(orbs, delta, bias)


def shards(cholesky, green, aux_field, walker_orbitals):
    vecs, rows, orbitals = cholesky.shape
    walkers = green.shape[0]
    occupied = walker_orbitals.shape[2]
    flat = rows * orbitals
    walk = walkers // NQ
    own_walk = walk // 8
    a_all, b_all = flat * SHARE // 16, flat * (16 - SHARE) // 16
    aux = aux_field.reshape(8, 2, walkers, vecs)
    orbs = walker_orbitals.reshape(NQ, 8, own_walk, rows, occupied)
    vmem = pltpu.VMEM
    scratch = [
        vmem((8, vecs // 8, rows, orbitals), BF),
        vmem((walkers, rows, orbitals), BF),
        vmem((2 * vecs, flat), BF),
        vmem((NQ, 4, 2, walk, flat), BF),
        vmem((NQ, 8, walk, 2 * vecs), BF),
        vmem((NQ, 7, walk, 2 * vecs), BF),
        vmem((NQ, 8, walk, 2 * vecs), BF),
        vmem((2, 8, walkers, vecs), F32),
        vmem((NQ, 8 * walk, 2 * vecs), BF),
        vmem((NQ, 4, 2, walk, flat), BF),
        vmem((NQ, 4, walk, a_all), BF),
        vmem((NQ, 2, walk, b_all // 2), BF),
        vmem((NQ, 2, walk, b_all // 2), BF),
        vmem((NQ, 2, walk, b_all), BF),
        vmem((NQ, 2, walk, b_all), BF),
        vmem((NQ, walk, b_all), BF),
        vmem((NQ, walk, a_all // 2), BF),
        vmem((NQ, walk, a_all // 2), BF),
        vmem((NQ, walk, a_all), BF),
        vmem((NQ, walk, a_all), BF),
        vmem((NQ, walk, rows, orbitals), BF),
        vmem((NQ, own_walk, 8 * rows, orbitals), BF),
        vmem((NQ, own_walk, 8 * rows, occupied), BF),
        vmem((NQ, own_walk, 8 * rows, occupied), BF),
        pltpu.SemaphoreType.DMA((160,)),
        pltpu.SemaphoreType.DMA((160,)),
        pltpu.SemaphoreType.DMA((16,)),
    ]
    anywhere = pl.BlockSpec(memory_space=pl.ANY)
    bias, delta = pl.pallas_call(
        kernel,
        out_shape=(
            jax.ShapeDtypeStruct((8, 2, walkers, vecs), BF),
            jax.ShapeDtypeStruct(orbs.shape, BF),
        ),
        in_specs=[anywhere] * 4,
        out_specs=(anywhere, anywhere),
        scratch_shapes=scratch,
        compiler_params=pltpu.CompilerParams(
            collective_id=0, has_side_effects=True, vmem_limit_bytes=60 * 2**20
        ),
    )(cholesky, green, aux, orbs)
    return widen(walker_orbitals, delta.reshape(walker_orbitals.shape), bias.reshape(aux_field.shape))


def solution(mesh):
    return jax.shard_map(
        shards,
        mesh=mesh,
        in_specs=(
            P("blk", "rows", None),
            P("blk", "rows", None),
            P(None, "blk"),
            P("blk", "rows", None),
        ),
        out_specs=(P("blk", "rows", None), P(None, "blk")),
        check_vma=False,
    )
```
